32 devices in a mesh: parts: 2 (over x), wide: 16 (over z, y, core).
Axes of the slice: x: 2, y: 2, z: 4, core: 2. Of those that a mesh axis runs over, the one named last changes fastest.
Arguments:
- tokens: bfloat16 [8192, 2048], P(('parts', 'wide')), parts along dimension 0, may hold values from -6 to 6
- token_group: int32 [8192], P(('parts', 'wide')), parts along dimension 0, may hold values from 0 to 255, as said below
- group_experts: int32 [512, 1], P(('parts', 'wide')), parts along dimension 0, may hold values from -1 to 15, as said below
- route_ids: int32 [8192, 8], P(('parts', 'wide')), parts along dimension 0, may hold values from 0 to 15, as said below
- route_gates: float32 [8192, 8], P(('parts', 'wide')), parts along dimension 0, may hold values from 0.1 to 1
- w_gate: bfloat16 [16, 2048, 768], P('wide'), may hold values from -0.125 to 0.125
- w_up: bfloat16 [16, 2048, 768], P('wide'), may hold values from -0.125 to 0.125
- w_down: bfloat16 [16, 768, 2048], P('wide'), may hold values from -0.21875 to 0.21875
Outputs:
- mixed: bfloat16 [8192, 2048], P(('parts', 'wide')), parts along dimension 0
The draws below stay inside these ranges and needn't reach their ends.
There are 2 independent parts, one for each index of `parts`. The reference program is written for one: setup_inputs(seed, part) draws one part's arguments, and reference() takes and returns one part's arrays. A program takes and returns all parts, laid end to end along the dimension named above; an argument that names none is the same for every part. Nothing has to cross between parts.
Inputs may be any that keep to these rules, and one draw needn't show every extreme that they name: `token_group`: Nondecreasing. The 256 tokens of index d of wide form groups d * 16 to d * 16 + 15, each a run of 1 to 24 tokens; on every index one group has exactly 24 tokens. `group_experts`: row g holds 2 to 1 distinct experts in its first entries and -1 after them; the groups of one index of wide list disjoint experts; every index has a group of 1 expert holding 24 tokens. Hence at most 24 tokens of one index of wide are kept for one expert, and one expert gets exactly 24 from every index. `route_ids`: each row names 8 distinct experts, among them every expert listed for the token's group.
All inputs are finite; a program needn't handle non-finite values.
Results may differ from the reference program's by a relative error of at most 0.0058.
Values may be sent and summed in bfloat16 or wider, within the bound.
No kernel may reach another device: no remote copies, remote signals or barrier semaphores. Data moves between devices by JAX's collectives and lax.ppermute only.
A program may use at most 128 MiB of HBM per device.

```python
import math
import jax
import jax.numpy as jnp
from jax import lax

D = 2048
FF = 768
TOP = 8
GRP_DEV = 16
TOK_DEV = 256
CAP = 24
EXPERTS = 16
LIST = 1
GROUPS = 256
TOKENS = 4096
N_WIDE = 16


def layout(key):
    base = jax.random.fold_in(key, 4242)
    devices = GROUPS // GRP_DEV
    rest = TOK_DEV - CAP
    per = rest // (GRP_DEV - 1)
    extra = rest % (GRP_DEV - 1)
    reach = max(0, min(per - 1, CAP - per - 1))
    pairs = (GRP_DEV - 1) // 2
    others = per + (jnp.arange(GRP_DEV - 1) < extra).astype(jnp.int32)
    shifts = jax.random.randint(jax.random.fold_in(base, 1), (devices, pairs), -reach, reach + 1)
    moved = jnp.stack([shifts, -shifts], axis=2).reshape(devices, 2 * pairs)
    moved = jnp.pad(moved, ((0, 0), (0, GRP_DEV - 1 - 2 * pairs)))
    sizes_first = jnp.concatenate([jnp.full((devices, 1), CAP, jnp.int32), others[None, :] + moved], axis=1)
    group_iota = jnp.arange(GRP_DEV, dtype=jnp.int32)
    order = jnp.argsort(jax.random.randint(jax.random.fold_in(base, 2), (devices, GRP_DEV), 0, 4096) * GRP_DEV + group_iota[None, :], axis=1)
    sizes = jnp.take_along_axis(sizes_first, order, axis=1)
    widest = jnp.argmax((order == 0).astype(jnp.int32), axis=1).astype(jnp.int32)
    ends = jnp.cumsum(sizes, axis=1)
    position = jnp.arange(TOK_DEV, dtype=jnp.int32)
    local = jnp.sum((ends[:, None, :] <= position[None, :, None]).astype(jnp.int32), axis=2)
    token_group = (local + jnp.arange(devices, dtype=jnp.int32)[:, None] * GRP_DEV).reshape(-1).astype(jnp.int32)
    counts = jax.random.randint(jax.random.fold_in(base, 3), (devices, GRP_DEV), max(1, LIST // 2), LIST + 1)
    counts = jnp.where(group_iota[None, :] == widest[:, None], LIST, counts)
    popular = jax.random.permutation(jax.random.fold_in(base, 4), EXPERTS).astype(jnp.int32)
    rank = jnp.argsort(popular).astype(jnp.int32)
    expert_iota = jnp.arange(EXPERTS, dtype=jnp.int32)
    score = jax.random.randint(jax.random.fold_in(base, 5), (devices, EXPERTS), 0, 4096) * (rank[None, :] + 4) // 4
    score = jnp.where(expert_iota[None, :] == popular[0], -1, score * EXPERTS + expert_iota[None, :])
    pick = jnp.argsort(score, axis=1).astype(jnp.int32)
    turn = jnp.where(group_iota[None, :] == widest[:, None], 0, group_iota[None, :] + (group_iota[None, :] < widest[:, None]).astype(jnp.int32))
    offset = jnp.sum(counts[:, None, :] * (turn[:, None, :] < turn[:, :, None]).astype(jnp.int32), axis=2)
    slot = jnp.arange(LIST, dtype=jnp.int32)
    where_at = jnp.minimum(offset[:, :, None] + slot[None, None, :], EXPERTS - 1)
    named = jnp.take_along_axis(pick, where_at.reshape(devices, GRP_DEV * LIST), axis=1).reshape(devices, GRP_DEV, LIST)
    group_experts = jnp.where(slot[None, None, :] < counts[:, :, None], named, -1).reshape(GROUPS, LIST).astype(jnp.int32)
    return (token_group, group_experts)


def draw_token_group(key, part):
    return layout(key)[0]


def draw_group_experts(key, part):
    return layout(key)[1]


def draw_route_ids(key, part):
    token_group, group_experts = layout(key)
    base = jax.random.fold_in(key, 777)
    lists = group_experts[token_group]
    expert_iota = jnp.arange(EXPERTS, dtype=jnp.int32)
    member = jnp.any(lists[:, :, None] == expert_iota[None, None, :], axis=1).astype(jnp.int32)
    score = jax.random.randint(jax.random.fold_in(base, 1), (TOKENS, EXPERTS), 0, 4096) * EXPERTS + expert_iota[None, :] - member * (4096 * EXPERTS)
    chosen = jnp.argsort(score, axis=1)[:, :TOP]
    shuffle = jnp.argsort(jax.random.randint(jax.random.fold_in(base, 2), (TOKENS, TOP), 0, 4096) * TOP + jnp.arange(TOP)[None, :], axis=1)
    return jnp.take_along_axis(chosen, shuffle, axis=1).astype(jnp.int32)


def shard_levels(stream_key, extent, shards, low, high):
    level, own = 1.0, jax.random.fold_in(stream_key, 6)
    for axis_at, blocks in shards:
        draws = jnp.exp(jax.random.uniform(jax.random.fold_in(own, axis_at), (blocks,), jnp.float32, low / len(shards), high / len(shards)))
        level = level * jnp.repeat(draws, extent[axis_at] // blocks).reshape([-1 if axis == axis_at else 1 for axis in range(len(extent))])
    return level


def normal_values(key, extent, deviation, most, pieces=(), kind=jnp.bfloat16):
    values = deviation * jax.random.normal(key, extent, jnp.float32)
    if pieces:
        values = values * shard_levels(key, extent, pieces, -0.22, 0.18)
    return jnp.clip(values, -most, most).astype(kind)


def setup_inputs(seed: int = 0, part: int = 0) -> dict:
    arg_keys = jax.random.split(jax.random.key(seed), 9)
    own_keys = jax.random.split(jax.random.fold_in(arg_keys[8], part), 9)
    tokens = normal_values(own_keys[0], (TOKENS, D), 1.0, 6.0, ((0, 16),))
    token_group = draw_token_group(jax.random.fold_in(jax.random.fold_in(arg_keys[8], part), 71), part)
    group_experts = draw_group_experts(jax.random.fold_in(jax.random.fold_in(arg_keys[8], part), 71), part)
    route_ids = draw_route_ids(jax.random.fold_in(jax.random.fold_in(arg_keys[8], part), 71), part)
    route_gates = jnp.clip(jnp.exp(math.log(1.0) - 2.3025851 * jax.random.uniform(own_keys[4], (TOKENS, TOP), jnp.float32) ** shard_levels(own_keys[4], (TOKENS, TOP), ((0, 16),), -0.2, 0.2)), 0.1, 1.0)
    w_gate = normal_values(arg_keys[5], (EXPERTS, D, FF), D ** -0.5, 0.125, ((0, 16),))
    w_up = normal_values(arg_keys[6], (EXPERTS, D, FF), D ** -0.5, 0.125, ((0, 16),))
    w_down = normal_values(arg_keys[7], (EXPERTS, FF, D), FF ** -0.5, 0.21875, ((0, 16),))
    return {"tokens": tokens, "token_group": token_group, "group_experts": group_experts, "route_ids": route_ids, "route_gates": route_gates, "w_gate": w_gate, "w_up": w_up, "w_down": w_down}


def expert_rows(rows, gate_w, up_w, down_w):
    gate = jnp.dot(rows, gate_w, preferred_element_type=jnp.float32)
    upper = jnp.dot(rows, up_w, preferred_element_type=jnp.float32)
    hidden = (jax.nn.silu(gate) * upper).astype(jnp.bfloat16)
    return jnp.dot(hidden, down_w, preferred_element_type=jnp.float32).astype(jnp.bfloat16)


def reference(tokens, token_group, group_experts, route_ids, route_gates, w_gate, w_up, w_down):
    group_iota = jnp.arange(GROUPS, dtype=jnp.int32)
    sizes = jnp.sum((token_group[:, None] == group_iota[None, :]).astype(jnp.int32), axis=0)
    starts = jnp.cumsum(sizes) - sizes
    sizes_dev = sizes.reshape(N_WIDE, GRP_DEV)
    starts_dev = starts.reshape(N_WIDE, GRP_DEV)
    lists = group_experts.reshape(N_WIDE, GRP_DEV, LIST)
    slot_iota = jnp.arange(CAP, dtype=jnp.int32)

    def one_expert(total, expert):
        listed = jnp.any(lists == expert, axis=2).astype(jnp.int32)
        run_start = jnp.sum(listed * starts_dev, axis=1)
        run_size = jnp.sum(listed * sizes_dev, axis=1)
        rows = run_start[:, None] + slot_iota[None, :]
        live = (slot_iota[None, :] < run_size[:, None]).reshape(-1)
        rows = jnp.minimum(rows, TOKENS - 1).reshape(-1).astype(jnp.int32)
        picked = tokens[rows]
        result = expert_rows(picked, w_gate[expert], w_up[expert], w_down[expert])
        weight = jnp.sum(jnp.where(route_ids[rows] == expert, route_gates[rows], jnp.zeros((), route_gates.dtype)), axis=1)
        weight = jnp.where(live, weight, jnp.zeros((), weight.dtype))
        return total.at[rows].add(weight[:, None] * result.astype(weight.dtype)), None

    start_total = jnp.zeros((TOKENS, D), route_gates.dtype)
    total, unused = lax.scan(one_expert, start_total, jnp.arange(EXPERTS, dtype=jnp.int32))
    return total.astype(jnp.bfloat16)
```

```python
import functools

import jax
import jax.numpy as jnp
from jax import lax
from jax.experimental import pallas as pl
from jax.experimental.pallas import tpu as pltpu
from jax.sharding import PartitionSpec as P

CAP = 24
CHUNKS = (24,)


def bounds(chunks):
    at = 0
    out = []
    for rows in chunks:
        out.append((at, rows))
        at += rows
    return out


def token_slots(group_row, first_group, groups_here):
    tokens_here = group_row.shape[1]
    gid = lax.broadcasted_iota(jnp.int32, (groups_here, tokens_here), 0) + first_group
    starts = jnp.sum((group_row < gid).astype(jnp.int32), axis=1, keepdims=True)
    member = group_row == gid
    start = jnp.sum(jnp.where(member, starts, 0), axis=0, keepdims=True)
    slot = lax.broadcasted_iota(jnp.int32, (1, tokens_here), 1) - start
    return member, slot


def named_expert(member, lists, index):
    groups_here = member.shape[0]
    row = lists[index : index + 1, :]
    square = (groups_here, groups_here)
    diagonal = lax.broadcasted_iota(jnp.int32, square, 0) == lax.broadcasted_iota(jnp.int32, square, 1)
    column = jnp.sum(jnp.where(diagonal, jnp.broadcast_to(row, square), 0), axis=1, keepdims=True)
    return jnp.sum(jnp.where(member, column, 0), axis=0, keepdims=True)


def slot_hot(expert, slot, start, rows, owners):
    fits = (expert >= 0) & (slot >= start) & (slot < start + rows)
    key = jnp.where(fits, expert * rows + slot - start, -1)
    tokens_here = key.shape[1]
    return lax.broadcasted_iota(jnp.int32, (owners * rows, tokens_here), 0) == key


def pack_kernel(chunks, owners, me_ref, group_ref, lists_ref, tokens_ref, *refs):
    outs = refs[: len(chunks)]
    hots = refs[len(chunks) :]

    @pl.when(pl.program_id(0) == 0)
    def _():
        groups_here = lists_ref.shape[1]
        member, slot = token_slots(group_ref[...], me_ref[0] * groups_here, groups_here)
        experts = [named_expert(member, lists_ref[...], j) for j in range(lists_ref.shape[0])]
        for (start, rows), hot in zip(bounds(chunks), hots):
            total = slot_hot(experts[0], slot, start, rows, owners)
            for expert in experts[1:]:
                total = total | slot_hot(expert, slot, start, rows, owners)
            hot[...] = total.astype(jnp.float32).astype(jnp.bfloat16)

    for out, hot in zip(outs, hots):
        rows = jnp.dot(hot[...], tokens_ref[...], preferred_element_type=jnp.float32)
        out[...] = rows.astype(jnp.bfloat16)


def pack(me, group_row, lists, tokens, owners, chunks):
    count, width = tokens.shape
    block = min(width, 512)
    whole = lambda shape: pl.BlockSpec(shape, lambda i, *_: (0, 0))
    column = lambda rows: pl.BlockSpec((rows, block), lambda i, *_: (0, i))
    return pl.pallas_call(
        functools.partial(pack_kernel, chunks, owners),
        grid_spec=pltpu.PrefetchScalarGridSpec(
            num_scalar_prefetch=1,
            grid=(width // block,),
            in_specs=[whole(group_row.shape), whole(lists.shape), column(count)],
            out_specs=[column(owners * rows) for rows in chunks],
            scratch_shapes=[pltpu.VMEM((owners * rows, count), jnp.bfloat16) for rows in chunks],
        ),
        out_shape=[jax.ShapeDtypeStruct((owners * rows, width), jnp.bfloat16) for rows in chunks],
        cost_estimate=pl.CostEstimate(
            flops=2 * owners * sum(chunks) * count * width,
            bytes_accessed=2 * width * (count + owners * sum(chunks)),
            transcendentals=0,
        ),
        name="pack",
    )(me, group_row, lists, tokens)


def mix_kernel(chunks, owners, me_ref, group_ref, lists_ref, ids_ref, gates_ref, *refs):
    backs = refs[: len(chunks)]
    out_ref = refs[len(chunks)]
    hots = refs[len(chunks) + 1 : 2 * len(chunks) + 1]
    weight_ref = refs[2 * len(chunks) + 1]
    lists_long = lists_ref.shape[0]

    @pl.when(pl.program_id(0) == 0)
    def _():
        groups_here = lists_ref.shape[1]
        member, slot = token_slots(group_ref[...], me_ref[0] * groups_here, groups_here)
        for j in range(lists_long):
            expert = named_expert(member, lists_ref[...], j)
            gate = jnp.sum(jnp.where(ids_ref[...] == expert, gates_ref[...], 0.0), axis=0, keepdims=True)
            weight_ref[j] = jnp.transpose(jnp.broadcast_to(gate, (128, gate.shape[1])))
            for (start, rows), hot in zip(bounds(chunks), hots):
                picks = slot_hot(expert, slot, start, rows, owners).astype(jnp.float32)
                hot[j] = jnp.transpose(picks).astype(jnp.bfloat16)

    total = None
    for j in range(lists_long):
        rows = None
        for back, hot in zip(backs, hots):
            part = jnp.dot(hot[j], back[...], preferred_element_type=jnp.float32)
            rows = part if rows is None else rows + part
        weight = jnp.tile(weight_ref[j], (1, rows.shape[1] // 128))
        total = rows * weight if total is None else total + rows * weight
    out_ref[...] = total.astype(jnp.bfloat16)


def mix(me, group_row, lists, ids, gates, backs, owners, chunks):
    count = group_row.shape[1]
    width = backs[0].shape[1]
    block = min(width, 512)
    whole = lambda shape: pl.BlockSpec(shape, lambda i, *_: (0, 0))
    column = lambda rows: pl.BlockSpec((rows, block), lambda i, *_: (0, i))
    lists_long = lists.shape[0]
    return pl.pallas_call(
        functools.partial(mix_kernel, chunks, owners),
        grid_spec=pltpu.PrefetchScalarGridSpec(
            num_scalar_prefetch=1,
            grid=(width // block,),
            in_specs=[whole(group_row.shape), whole(lists.shape), whole(ids.shape), whole(gates.shape)]
            + [column(owners * rows) for rows in chunks],
            out_specs=column(count),
            scratch_shapes=[pltpu.VMEM((lists_long, count, owners * rows), jnp.bfloat16) for rows in chunks]
            + [pltpu.VMEM((lists_long, count, 128), jnp.float32)],
        ),
        out_shape=jax.ShapeDtypeStruct((count, width), jnp.bfloat16),
        cost_estimate=pl.CostEstimate(
            flops=2 * owners * sum(chunks) * count * width,
            bytes_accessed=2 * width * (count + owners * sum(chunks)),
            transcendentals=0,
        ),
        name="mix",
    )(me, group_row, lists, ids, gates, *backs)


def swiglu(rows, gate_w, up_w, down_w):
    gate = jnp.dot(rows, gate_w, preferred_element_type=jnp.float32)
    upper = jnp.dot(rows, up_w, preferred_element_type=jnp.float32)
    hidden = (jax.nn.silu(gate) * upper).astype(jnp.bfloat16)
    return jnp.dot(hidden, down_w, preferred_element_type=jnp.float32).astype(jnp.bfloat16)


def exchange(rows, owners):
    blocks = rows.reshape(owners, -1, rows.shape[1])
    return lax.all_to_all(blocks, "wide", split_axis=0, concat_axis=0, tiled=True).reshape(rows.shape)


def on_device(tokens, token_group, group_experts, route_ids, route_gates, w_gate, w_up, w_down):
    owners = lax.axis_size("wide")
    me = lax.axis_index("wide").reshape(1)
    group_row = token_group.reshape(1, -1)
    lists = group_experts.T
    sent = pack(me, group_row, lists, tokens, owners, CHUNKS)
    arrived = [exchange(rows, owners) for rows in sent]
    results = [swiglu(rows, w_gate[0], w_up[0], w_down[0]) for rows in arrived]
    backs = [exchange(rows, owners) for rows in results]
    return mix(me, group_row, lists, route_ids.T, route_gates.T, backs, owners, CHUNKS)


def solution(mesh):
    in_specs = (
        P(("parts", "wide"), None),
        P(("parts", "wide")),
        P(("parts", "wide"), None),
        P(("parts", "wide"), None),
        P(("parts", "wide"), None),
        P("wide", None, None),
        P("wide", None, None),
        P("wide", None, None),
    )
    out_specs = P(("parts", "wide"), None)
    return jax.shard_map(
        on_device, mesh=mesh, in_specs=in_specs, out_specs=out_specs, check_vma=False
    )
```

```python
import functools

import jax
import jax.numpy as jnp
from jax import lax
from jax.experimental import pallas as pl
from jax.experimental.pallas import tpu as pltpu
from jax.sharding import PartitionSpec as P


CAP = 24
IN_BLOCK = 256
OUT_BLOCK = 1024
COPY_BLOCK = 512
VMEM_BYTES = 67043328
ANY = pl.BlockSpec(memory_space=pl.ANY)
HBM = pl.BlockSpec(memory_space=pltpu.HBM)
VMEM = pl.BlockSpec(memory_space=pltpu.VMEM)


def token_slots(group_row, first_group, groups_here):
    tokens_here = group_row.shape[1]
    gid = lax.broadcasted_iota(jnp.int32, (groups_here, tokens_here), 0) + first_group
    starts = jnp.sum((group_row < gid).astype(jnp.int32), axis=1, keepdims=True)
    member = group_row == gid
    start = jnp.sum(jnp.where(member, starts, 0), axis=0, keepdims=True)
    slot = lax.broadcasted_iota(jnp.int32, (1, tokens_here), 1) - start
    return member, slot


def named_expert(member, lists, index):
    groups_here = member.shape[0]
    row = lists[index : index + 1, :]
    square = (groups_here, groups_here)
    diagonal = lax.broadcasted_iota(jnp.int32, square, 0) == lax.broadcasted_iota(jnp.int32, square, 1)
    column = jnp.sum(jnp.where(diagonal, jnp.broadcast_to(row, square), 0), axis=1, keepdims=True)
    return jnp.sum(jnp.where(member, column, 0), axis=0, keepdims=True)


def slot_hot(expert, slot, me, first, count, owners):
    place = ((expert ^ me) - first) & (owners - 1)
    key = jnp.where(expert >= 0, place * CAP + slot, -1)
    return lax.broadcasted_iota(jnp.int32, (count * CAP, key.shape[1]), 0) == key


def roomy(scratch):
    return scratch + 8 * 1024 * 1024


def block_rows(index):
    return pl.ds(index * CAP, CAP)


def column_blocks(width):
    block = min(width, COPY_BLOCK)
    return [pl.ds(at, block) for at in range(0, width, block)]


def start_all(copies):
    for copy in copies:
        copy.start()


def wait_all(copies):
    for copy in copies:
        copy.wait()


def token_loads(tokens_hbm, tokens_ref, sems):
    return [
        pltpu.make_async_copy(tokens_hbm.at[:, cols], tokens_ref.at[:, cols], sems.at[i])
        for i, cols in enumerate(column_blocks(tokens_ref.shape[1]))
    ]


def pack_rows(experts, slot, me, first, owners, loads, tokens_ref, outs):
    total = None
    for expert in experts:
        picks = slot_hot(expert, slot, me, first, len(outs), owners)
        total = picks if total is None else total | picks
    hot = total.astype(jnp.float32).astype(jnp.bfloat16)
    for load, cols in zip(loads, column_blocks(tokens_ref.shape[1])):
        load.wait()
        rows = jnp.dot(hot, tokens_ref[:, cols], preferred_element_type=jnp.float32)
        for i, out in enumerate(outs):
            out[:, cols] = rows[i * CAP : (i + 1) * CAP].astype(jnp.bfloat16)


def pack_kernel(owners, first, count, group_ref, lists_ref, tokens_hbm, *refs):
    outs = refs[:count]
    tokens_ref, in_sems = refs[count:]
    loads = token_loads(tokens_hbm, tokens_ref, in_sems)
    start_all(loads)
    me = lax.axis_index("wide")
    groups_here = lists_ref.shape[1]
    member, slot = token_slots(group_ref[...], me * groups_here, groups_here)
    experts = [named_expert(member, lists_ref[...], j) for j in range(lists_ref.shape[0])]
    pack_rows(experts, slot, me, first, owners, loads, tokens_ref, outs)


def pack(group_row, lists, tokens, owners, first, count):
    height, width = tokens.shape
    return pl.pallas_call(
        functools.partial(pack_kernel, owners, first, count),
        in_specs=[VMEM, VMEM, ANY],
        out_specs=[VMEM] * count,
        scratch_shapes=[
            pltpu.VMEM((height, width), jnp.bfloat16),
            pltpu.SemaphoreType.DMA((len(column_blocks(width)),)),
        ],
        out_shape=[pltpu.VMEM((CAP, width), jnp.bfloat16)] * count,
        cost_estimate=pl.CostEstimate(
            flops=2 * count * CAP * height * width,
            bytes_accessed=2 * width * (height + count * CAP),
            transcendentals=0,
        ),
        name="pack",
    )(group_row, lists, tokens)


def plan_kernel(owners, first, count, spans, group_ref, lists_ref, ids_ref, gates_ref, tokens_hbm, *refs):
    sources, refs = refs[:3], refs[3:]
    outs, refs = refs[:count], refs[count:]
    hots, refs = refs[: len(spans)], refs[len(spans) :]
    weight_ref, kept, (tokens_ref, in_sems, kept_sems) = refs[0], refs[1:4], refs[4:]
    loads = token_loads(tokens_hbm, tokens_ref, in_sems)
    keeps = [
        pltpu.make_async_copy(source, target, kept_sems.at[i]) for i, (source, target) in enumerate(zip(sources, kept))
    ]
    start_all(loads)
    start_all(keeps)
    me = lax.axis_index("wide")
    groups_here = lists_ref.shape[1]
    member, slot = token_slots(group_ref[...], me * groups_here, groups_here)
    experts = [named_expert(member, lists_ref[...], j) for j in range(lists_ref.shape[0])]
    pack_rows(experts, slot, me, first, owners, loads, tokens_ref, outs)
    for j, expert in enumerate(experts):
        gate = jnp.sum(jnp.where(ids_ref[...] == expert, gates_ref[...], 0.0), axis=0, keepdims=True)
        weight_ref[j] = jnp.transpose(jnp.broadcast_to(gate, (128, gate.shape[1])))
        for (start, length), hot in zip(spans, hots):
            picks = slot_hot(expert, slot, me, start, length, owners).astype(jnp.float32)
            hot[j] = jnp.transpose(picks).astype(jnp.bfloat16)
    wait_all(keeps)


def plan(group_row, lists, ids, gates, tokens, weights, owners, first, count, spans):
    height, width = tokens.shape
    lists_long = lists.shape[0]
    return pl.pallas_call(
        functools.partial(plan_kernel, owners, first, count, spans),
        in_specs=[VMEM] * 4 + [ANY] * 4,
        out_specs=[VMEM] * (count + len(spans) + 4),
        scratch_shapes=[
            pltpu.VMEM((height, width), jnp.bfloat16),
            pltpu.SemaphoreType.DMA((len(column_blocks(width)),)),
            pltpu.SemaphoreType.DMA((len(weights),)),
        ],
        out_shape=[pltpu.VMEM((CAP, width), jnp.bfloat16)] * count
        + [pltpu.VMEM((lists_long, height, length * CAP), jnp.bfloat16) for _, length in spans]
        + [pltpu.VMEM((lists_long, height, 128), jnp.float32)]
        + [pltpu.VMEM(weight.shape, weight.dtype) for weight in weights],
        cost_estimate=pl.CostEstimate(
            flops=2 * count * CAP * height * width,
            bytes_accessed=sum(2 * weight.size for weight in weights),
            transcendentals=0,
        ),
        compiler_params=pltpu.CompilerParams(
            vmem_limit_bytes=VMEM_BYTES
            - sum(2 * weight.size for weight in weights)
            - 4 * owners * CAP * width
            - lists_long * height * (2 * owners * CAP + 512)
        ),
        name="plan",
    )(group_row, lists, ids, gates, tokens, *weights)


def gather_blocks(blocks, rows_ref):
    for i, block in enumerate(blocks):
        rows_ref[block_rows(i)] = block[...]


def select_kernel(count, added, hot_ref, *refs):
    blocks, before, (out_ref, rows_ref) = refs[:count], refs[count : count + added], refs[count + added :]
    gather_blocks(blocks, rows_ref)
    for j in range(hot_ref.shape[0]):
        for cols in column_blocks(rows_ref.shape[1]):
            picked = jnp.dot(hot_ref[j], rows_ref[:, cols], preferred_element_type=jnp.float32)
            for other in before:
                picked = picked + other[j, :, cols].astype(jnp.float32)
            out_ref[j, :, cols] = picked.astype(jnp.bfloat16)


def select(hot, blocks, before):
    lists_long, height = hot.shape[:2]
    width = blocks[0].shape[1]
    return pl.pallas_call(
        functools.partial(select_kernel, len(blocks), len(before)),
        in_specs=[VMEM] * (1 + len(blocks) + len(before)),
        out_specs=VMEM,
        scratch_shapes=[pltpu.VMEM((len(blocks) * CAP, width), jnp.bfloat16)],
        out_shape=pltpu.VMEM((lists_long, height, width), jnp.bfloat16),
        cost_estimate=pl.CostEstimate(
            flops=2 * hot.size * width, bytes_accessed=2 * len(blocks) * CAP * width, transcendentals=0
        ),
        compiler_params=pltpu.CompilerParams(
            vmem_limit_bytes=roomy(2 * (2 * len(blocks) * CAP * width + hot.size + 2 * lists_long * height * width))
        ),
        name="select",
    )(hot, *blocks, *before)


def mix_kernel(count, picked_ref, hot_ref, weight_ref, *refs):
    blocks = refs[:count]
    out_hbm, rows_ref, out_ref, sems = refs[count:]
    gather_blocks(blocks, rows_ref)
    stores = []
    for index, cols in enumerate(column_blocks(rows_ref.shape[1])):
        total = None
        for j in range(hot_ref.shape[0]):
            part = jnp.dot(hot_ref[j], rows_ref[:, cols], preferred_element_type=jnp.float32)
            part = part + picked_ref[j, :, cols].astype(jnp.float32)
            part = part * jnp.tile(weight_ref[j], (1, part.shape[1] // 128))
            total = part if total is None else total + part
        out_ref[:, cols] = total.astype(jnp.bfloat16)
        stores.append(pltpu.make_async_copy(out_ref.at[:, cols], out_hbm.at[:, cols], sems.at[index]))
        stores[-1].start()
    wait_all(stores)


def mix(picked, hot, weight, blocks):
    _, height, width = picked.shape
    return pl.pallas_call(
        functools.partial(mix_kernel, len(blocks)),
        in_specs=[VMEM] * (3 + len(blocks)),
        out_specs=ANY,
        scratch_shapes=[
            pltpu.VMEM((len(blocks) * CAP, width), jnp.bfloat16),
            pltpu.VMEM((height, width), jnp.bfloat16),
            pltpu.SemaphoreType.DMA((len(column_blocks(width)),)),
        ],
        out_shape=jax.ShapeDtypeStruct((height, width), jnp.bfloat16),
        cost_estimate=pl.CostEstimate(
            flops=2 * hot.size * width, bytes_accessed=2 * height * width, transcendentals=0
        ),
        compiler_params=pltpu.CompilerParams(
            vmem_limit_bytes=roomy(
                2 * (2 * len(blocks) * CAP * width + height * width + hot.size + picked.size) + 4 * weight.size
            )
        ),
        name="mix",
    )(picked, hot, weight, *blocks)


def expert_kernel(count, narrow, wide, *refs):
    blocks = refs[:count]
    gate_ref, up_ref, down_ref = refs[count : count + 3]
    outs = refs[count + 3 : 2 * count + 3]
    rows_ref, hidden_ref = refs[2 * count + 3 :]
    width, inner = gate_ref.shape[1:]
    for i, block in enumerate(blocks):
        rows_ref[block_rows(i)] = block[...]
    for at in range(0, inner, narrow):
        cols = pl.ds(at, narrow)
        both = jnp.concatenate([gate_ref[0, :, cols], up_ref[0, :, cols]], axis=1)
        mixed = jnp.dot(rows_ref[...], both, preferred_element_type=jnp.float32)
        hidden = jax.nn.silu(mixed[:, :narrow]) * mixed[:, narrow:]
        hidden_ref[:, cols] = hidden.astype(jnp.bfloat16)
    for at in range(0, width, wide):
        cols = pl.ds(at, wide)
        result = jnp.dot(hidden_ref[...], down_ref[0, :, cols], preferred_element_type=jnp.float32)
        for i, out in enumerate(outs):
            out[:, cols] = result[i * CAP : (i + 1) * CAP].astype(jnp.bfloat16)


def expert(blocks, w_gate, w_up, w_down):
    count = len(blocks)
    width, inner = w_gate.shape[1:]
    narrow = min(inner, IN_BLOCK)
    wide = min(width, OUT_BLOCK)
    return pl.pallas_call(
        functools.partial(expert_kernel, count, narrow, wide),
        in_specs=[VMEM] * (count + 3),
        out_specs=[VMEM] * count,
        scratch_shapes=[
            pltpu.VMEM((count * CAP, width), jnp.bfloat16),
            pltpu.VMEM((count * CAP, inner), jnp.bfloat16),
        ],
        out_shape=[pltpu.VMEM((CAP, width), jnp.bfloat16)] * count,
        cost_estimate=pl.CostEstimate(
            flops=6 * count * CAP * width * inner,
            bytes_accessed=4 * count * CAP * width,
            transcendentals=count * CAP * inner,
        ),
        compiler_params=pltpu.CompilerParams(vmem_limit_bytes=roomy(count * CAP * (4 * width + 2 * inner))),
        name="expert",
    )(*blocks, w_gate, w_up, w_down)


def swap(block, shift, owners):
    if shift == 0:
        return block
    return lax.ppermute(block, "wide", [(i, i ^ shift) for i in range(owners)])


def shifts_of(owners):
    quarter = owners // 4
    return (
        list(range(2 * quarter, 3 * quarter)),
        list(range(3 * quarter, owners)),
        list(range(quarter, 2 * quarter)) + list(range(1, quarter)),
    )


def on_device(tokens, token_group, group_experts, route_ids, route_gates, w_gate, w_up, w_down):
    owners = lax.axis_size("wide")
    assert owners & (owners - 1) == 0 and owners >= 4
    group_row = token_group.reshape(1, -1)
    lists = group_experts.T
    far_a, far_b, near = shifts_of(owners)
    rest = far_b + sorted([0] + near)
    sent = dict(zip(far_a, pack(group_row, lists, tokens, owners, far_a[0], len(far_a))))
    spans = ((far_a[0], len(far_a)), (0, 1 + len(near)), (far_b[0], len(far_b)))
    made = plan(
        group_row,
        lists,
        route_ids.T,
        route_gates.T,
        tokens,
        (w_gate, w_up, w_down),
        owners,
        far_b[0],
        len(rest),
        spans,
    )
    sent.update(zip(rest, made[: len(rest)]))
    hot_a, hot_near, hot_b, weight, *weights = made[len(rest) :]
    arrived = {0: sent[0]}
    for shift in far_a + far_b + near:
        arrived[shift] = swap(sent[shift], shift, owners)
    backs = {}
    for part in (far_a, near + [0], far_b):
        results = expert([arrived[shift] for shift in part], *weights)
        for shift, result in zip(part, results):
            backs[shift] = swap(result, shift, owners)
    picked = select(hot_a, [backs[shift] for shift in far_a], [])
    picked = select(hot_near, [backs[shift] for shift in sorted([0] + near)], [picked])
    return mix(picked, hot_b, weight, [backs[shift] for shift in far_b])


def solution(mesh):
    in_specs = (
        P(("parts", "wide"), None),
        P(("parts", "wide")),
        P(("parts", "wide"), None),
        P(("parts", "wide"), None),
        P(("parts", "wide"), None),
        P("wide", None, None),
        P("wide", None, None),
        P("wide", None, None),
    )
    out_specs = P(("parts", "wide"), None)
    return jax.shard_map(
        on_device, mesh=mesh, in_specs=in_specs, out_specs=out_specs, check_vma=False
    )
```

```python
import functools

import jax
import jax.numpy as jnp
from jax import lax
from jax.experimental import pallas as pl
from jax.experimental.pallas import tpu as pltpu
from jax.sharding import PartitionSpec as P


CAP = 24
IN_BLOCK = 256
OUT_BLOCK = 1024
COPY_BLOCK = 512
VMEM_BYTES = 67043328
FIRST = ("f0", "f1")
BATCHES = (("f0", "f1"), ("n",), ("f2", "f3"))
STAGES = (("f0", "f1"), ("n",), ("f2", "f3"))
ANY = pl.BlockSpec(memory_space=pl.ANY)
HBM = pl.BlockSpec(memory_space=pltpu.HBM)
VMEM = pl.BlockSpec(memory_space=pltpu.VMEM)


def token_slots(group_row, first_group, groups_here):
    tokens_here = group_row.shape[1]
    gid = lax.broadcasted_iota(jnp.int32, (groups_here, tokens_here), 0) + first_group
    starts = jnp.sum((group_row < gid).astype(jnp.int32), axis=1, keepdims=True)
    member = group_row == gid
    start = jnp.sum(jnp.where(member, starts, 0), axis=0, keepdims=True)
    slot = lax.broadcasted_iota(jnp.int32, (1, tokens_here), 1) - start
    return member, slot


def named_expert(member, lists, index):
    groups_here = member.shape[0]
    row = lists[index : index + 1, :]
    square = (groups_here, groups_here)
    diagonal = lax.broadcasted_iota(jnp.int32, square, 0) == lax.broadcasted_iota(jnp.int32, square, 1)
    column = jnp.sum(jnp.where(diagonal, jnp.broadcast_to(row, square), 0), axis=1, keepdims=True)
    return jnp.sum(jnp.where(member, column, 0), axis=0, keepdims=True)


def slot_hot(expert, slot, me, first, count, owners):
    place = ((expert ^ me) - first) & (owners - 1)
    key = jnp.where(expert >= 0, place * CAP + slot, -1)
    return lax.broadcasted_iota(jnp.int32, (count * CAP, key.shape[1]), 0) == key


def roomy(scratch):
    return scratch + 8 * 1024 * 1024


def block_rows(index):
    return pl.ds(index * CAP, CAP)


def column_blocks(width):
    block = min(width, COPY_BLOCK)
    return [pl.ds(at, block) for at in range(0, width, block)]


def start_all(copies):
    for copy in copies:
        copy.start()


def wait_all(copies):
    for copy in copies:
        copy.wait()


def pack_rows(experts, slot, me, first, owners, load, tokens_ref, outs):
    total = None
    for expert in experts:
        picks = slot_hot(expert, slot, me, first, len(outs), owners)
        total = picks if total is None else total | picks
    hot = total.astype(jnp.float32).astype(jnp.bfloat16)
    load.wait()
    for cols in column_blocks(tokens_ref.shape[1]):
        rows = jnp.dot(hot, tokens_ref[:, cols], preferred_element_type=jnp.float32)
        for i, out in enumerate(outs):
            out[:, cols] = rows[i * CAP : (i + 1) * CAP].astype(jnp.bfloat16)


def pack_kernel(owners, first, count, group_hbm, lists_hbm, tokens_hbm, *refs):
    outs = refs[:count]
    group_ref, lists_ref, tokens_ref, sems = refs[count:]
    pairs = ((group_hbm, group_ref), (lists_hbm, lists_ref), (tokens_hbm, tokens_ref))
    loads = [pltpu.make_async_copy(source, target, sems.at[i]) for i, (source, target) in enumerate(pairs)]
    start_all(loads)
    wait_all(loads[:2])
    me = lax.axis_index("wide")
    groups_here = lists_ref.shape[1]
    member, slot = token_slots(group_ref[...], me * groups_here, groups_here)
    experts = [named_expert(member, lists_ref[...], j) for j in range(lists_ref.shape[0])]
    pack_rows(experts, slot, me, first, owners, loads[2], tokens_ref, outs)


def pack(group_row, lists, tokens, owners, first, count):
    height, width = tokens.shape
    return pl.pallas_call(
        functools.partial(pack_kernel, owners, first, count),
        in_specs=[ANY] * 3,
        out_specs=[VMEM] * count,
        scratch_shapes=[
            pltpu.VMEM(group_row.shape, group_row.dtype),
            pltpu.VMEM(lists.shape, lists.dtype),
            pltpu.VMEM((height, width), jnp.bfloat16),
            pltpu.SemaphoreType.DMA((3,)),
        ],
        out_shape=[pltpu.VMEM((CAP, width), jnp.bfloat16)] * count,
        cost_estimate=pl.CostEstimate(
            flops=2 * count * CAP * height * width,
            bytes_accessed=2 * width * (height + count * CAP),
            transcendentals=0,
        ),
        name="pack",
    )(group_row, lists, tokens)


def plan_kernel(owners, first, count, spans, group_ref, lists_ref, ids_ref, gates_ref, tokens_hbm, *refs):
    sources, refs = refs[:3], refs[3:]
    outs, refs = refs[:count], refs[count:]
    hots, refs = refs[: len(spans)], refs[len(spans) :]
    weight_ref, kept, (tokens_ref, token_sem, kept_sems) = refs[0], refs[1:4], refs[4:]
    load = pltpu.make_async_copy(tokens_hbm, tokens_ref, token_sem)
    keeps = [
        pltpu.make_async_copy(source, target, kept_sems.at[i]) for i, (source, target) in enumerate(zip(sources, kept))
    ]
    load.start()
    start_all(keeps)
    me = lax.axis_index("wide")
    groups_here = lists_ref.shape[1]
    member, slot = token_slots(group_ref[...], me * groups_here, groups_here)
    experts = [named_expert(member, lists_ref[...], j) for j in range(lists_ref.shape[0])]
    pack_rows(experts, slot, me, first, owners, load, tokens_ref, outs)
    for j, expert in enumerate(experts):
        gate = jnp.sum(jnp.where(ids_ref[...] == expert, gates_ref[...], 0.0), axis=0, keepdims=True)
        weight_ref[j] = jnp.transpose(jnp.broadcast_to(gate, (128, gate.shape[1])))
        for (start, length), hot in zip(spans, hots):
            picks = slot_hot(expert, slot, me, start, length, owners).astype(jnp.float32)
            hot[j] = jnp.transpose(picks).astype(jnp.bfloat16)
    wait_all(keeps)


def plan(group_row, lists, ids, gates, tokens, weights, owners, first, count, spans):
    height, width = tokens.shape
    lists_long = lists.shape[0]
    return pl.pallas_call(
        functools.partial(plan_kernel, owners, first, count, spans),
        in_specs=[VMEM] * 4 + [ANY] * 4,
        out_specs=[VMEM] * (count + len(spans) + 4),
        scratch_shapes=[
            pltpu.VMEM((height, width), jnp.bfloat16),
            pltpu.SemaphoreType.DMA,
            pltpu.SemaphoreType.DMA((len(weights),)),
        ],
        out_shape=[pltpu.VMEM((CAP, width), jnp.bfloat16)] * count
        + [pltpu.VMEM((lists_long, height, length * CAP), jnp.bfloat16) for _, length in spans]
        + [pltpu.VMEM((lists_long, height, 128), jnp.float32)]
        + [pltpu.VMEM(weight.shape, weight.dtype) for weight in weights],
        cost_estimate=pl.CostEstimate(
            flops=2 * count * CAP * height * width,
            bytes_accessed=sum(2 * weight.size for weight in weights),
            transcendentals=0,
        ),
        compiler_params=pltpu.CompilerParams(
            vmem_limit_bytes=VMEM_BYTES
            - sum(2 * weight.size for weight in weights)
            - 4 * owners * CAP * width
            - lists_long * height * (2 * owners * CAP + 512)
        ),
        name="plan",
    )(group_row, lists, ids, gates, tokens, *weights)


def gather_blocks(blocks, rows_ref):
    for i, block in enumerate(blocks):
        rows_ref[block_rows(i)] = block[...]


def select_kernel(count, added, hot_ref, *refs):
    blocks, before, (out_ref, rows_ref) = refs[:count], refs[count : count + added], refs[count + added :]
    gather_blocks(blocks, rows_ref)
    for j in range(hot_ref.shape[0]):
        for cols in column_blocks(rows_ref.shape[1]):
            picked = jnp.dot(hot_ref[j], rows_ref[:, cols], preferred_element_type=jnp.float32)
            for other in before:
                picked = picked + other[j, :, cols].astype(jnp.float32)
            out_ref[j, :, cols] = picked.astype(jnp.bfloat16)


def select(hot, blocks, before):
    lists_long, height = hot.shape[:2]
    width = blocks[0].shape[1]
    return pl.pallas_call(
        functools.partial(select_kernel, len(blocks), len(before)),
        in_specs=[VMEM] * (1 + len(blocks) + len(before)),
        out_specs=VMEM,
        scratch_shapes=[pltpu.VMEM((len(blocks) * CAP, width), jnp.bfloat16)],
        out_shape=pltpu.VMEM((lists_long, height, width), jnp.bfloat16),
        cost_estimate=pl.CostEstimate(
            flops=2 * hot.size * width, bytes_accessed=2 * len(blocks) * CAP * width, transcendentals=0
        ),
        compiler_params=pltpu.CompilerParams(
            vmem_limit_bytes=roomy(2 * (2 * len(blocks) * CAP * width + hot.size + 2 * lists_long * height * width))
        ),
        name="select",
    )(hot, *blocks, *before)


def mix_kernel(count, picked_ref, hot_ref, weight_ref, *refs):
    blocks = refs[:count]
    out_hbm, rows_ref, out_ref, sems = refs[count:]
    gather_blocks(blocks, rows_ref)
    stores = []
    for index, cols in enumerate(column_blocks(rows_ref.shape[1])):
        total = None
        for j in range(hot_ref.shape[0]):
            part = jnp.dot(hot_ref[j], rows_ref[:, cols], preferred_element_type=jnp.float32)
            part = part + picked_ref[j, :, cols].astype(jnp.float32)
            part = part * jnp.tile(weight_ref[j], (1, part.shape[1] // 128))
            total = part if total is None else total + part
        out_ref[:, cols] = total.astype(jnp.bfloat16)
        stores.append(pltpu.make_async_copy(out_ref.at[:, cols], out_hbm.at[:, cols], sems.at[index]))
        stores[-1].start()
    wait_all(stores)


def mix(picked, hot, weight, blocks):
    _, height, width = picked.shape
    return pl.pallas_call(
        functools.partial(mix_kernel, len(blocks)),
        in_specs=[VMEM] * (3 + len(blocks)),
        out_specs=ANY,
        scratch_shapes=[
            pltpu.VMEM((len(blocks) * CAP, width), jnp.bfloat16),
            pltpu.VMEM((height, width), jnp.bfloat16),
            pltpu.SemaphoreType.DMA((len(column_blocks(width)),)),
        ],
        out_shape=jax.ShapeDtypeStruct((height, width), jnp.bfloat16),
        cost_estimate=pl.CostEstimate(
            flops=2 * hot.size * width, bytes_accessed=2 * height * width, transcendentals=0
        ),
        compiler_params=pltpu.CompilerParams(
            vmem_limit_bytes=roomy(
                2 * (2 * len(blocks) * CAP * width + height * width + hot.size + picked.size) + 4 * weight.size
            )
        ),
        name="mix",
    )(picked, hot, weight, *blocks)


def expert_kernel(count, narrow, wide, *refs):
    blocks = refs[:count]
    gate_ref, up_ref, down_ref = refs[count : count + 3]
    outs = refs[count + 3 : 2 * count + 3]
    rows_ref, hidden_ref = refs[2 * count + 3 :]
    width, inner = gate_ref.shape[1:]
    for i, block in enumerate(blocks):
        rows_ref[block_rows(i)] = block[...]
    for at in range(0, inner, narrow):
        cols = pl.ds(at, narrow)
        both = jnp.concatenate([gate_ref[0, :, cols], up_ref[0, :, cols]], axis=1)
        mixed = jnp.dot(rows_ref[...], both, preferred_element_type=jnp.float32)
        hidden = jax.nn.silu(mixed[:, :narrow]) * mixed[:, narrow:]
        hidden_ref[:, cols] = hidden.astype(jnp.bfloat16)
    for at in range(0, width, wide):
        cols = pl.ds(at, wide)
        result = jnp.dot(hidden_ref[...], down_ref[0, :, cols], preferred_element_type=jnp.float32)
        for i, out in enumerate(outs):
            out[:, cols] = result[i * CAP : (i + 1) * CAP].astype(jnp.bfloat16)


def expert(blocks, w_gate, w_up, w_down):
    count = len(blocks)
    width, inner = w_gate.shape[1:]
    narrow = min(inner, IN_BLOCK)
    wide = min(width, OUT_BLOCK)
    return pl.pallas_call(
        functools.partial(expert_kernel, count, narrow, wide),
        in_specs=[VMEM] * (count + 3),
        out_specs=[VMEM] * count,
        scratch_shapes=[
            pltpu.VMEM((count * CAP, width), jnp.bfloat16),
            pltpu.VMEM((count * CAP, inner), jnp.bfloat16),
        ],
        out_shape=[pltpu.VMEM((CAP, width), jnp.bfloat16)] * count,
        cost_estimate=pl.CostEstimate(
            flops=6 * count * CAP * width * inner,
            bytes_accessed=4 * count * CAP * width,
            transcendentals=count * CAP * inner,
        ),
        compiler_params=pltpu.CompilerParams(vmem_limit_bytes=roomy(count * CAP * (4 * width + 2 * inner))),
        name="expert",
    )(*blocks, w_gate, w_up, w_down)


def swap(block, shift, owners):
    if shift == 0:
        return block
    return lax.ppermute(block, "wide", [(i, i ^ shift) for i in range(owners)])


def shifts_of(owners):
    half = owners // 2
    far = list(range(half, owners))
    sets = {f"f{i}": far[len(far) * i // 4 : len(far) * (i + 1) // 4] for i in range(4)}
    sets["n"] = list(range(half))
    return sets


def joined(sets, names):
    return [shift for name in names for shift in sets[name]]


def on_device(tokens, token_group, group_experts, route_ids, route_gates, w_gate, w_up, w_down):
    owners = lax.axis_size("wide")
    assert owners & (owners - 1) == 0 and owners >= 8
    group_row = token_group.reshape(1, -1)
    lists = group_experts.T
    sets = shifts_of(owners)
    first = joined(sets, FIRST)
    rest = [(first[-1] + 1 + i) % owners for i in range(owners - len(first))]
    stages = [joined(sets, names) for names in STAGES]
    sent = dict(zip(first, pack(group_row, lists, tokens, owners, first[0], len(first))))
    spans = tuple((stage[0], len(stage)) for stage in stages)
    made = plan(
        group_row,
        lists,
        route_ids.T,
        route_gates.T,
        tokens,
        (w_gate, w_up, w_down),
        owners,
        rest[0],
        len(rest),
        spans,
    )
    sent.update(zip(rest, made[: len(rest)]))
    hots, weight, weights = made[len(rest) : -4], made[-4], made[-3:]
    arrived = {shift: swap(sent[shift], shift, owners) for shift in range(owners)}
    backs = {}
    for names in BATCHES:
        part = joined(sets, names)
        results = expert([arrived[shift] for shift in part], *weights)
        for shift, result in zip(part, results):
            backs[shift] = swap(result, shift, owners)
    picked = []
    for hot, stage in zip(hots[:-1], stages):
        picked = [select(hot, [backs[shift] for shift in stage], picked)]
    return mix(picked[0], hots[-1], weight, [backs[shift] for shift in stages[-1]])


def solution(mesh):
    in_specs = (
        P(("parts", "wide"), None),
        P(("parts", "wide")),
        P(("parts", "wide"), None),
        P(("parts", "wide"), None),
        P(("parts", "wide"), None),
        P("wide", None, None),
        P("wide", None, None),
        P("wide", None, None),
    )
    out_specs = P(("parts", "wide"), None)
    return jax.shard_map(
        on_device, mesh=mesh, in_specs=in_specs, out_specs=out_specs, check_vma=False
    )
```

```python
import functools

import jax
import jax.numpy as jnp
from jax import lax
from jax.experimental import pallas as pl
from jax.experimental.pallas import tpu as pltpu
from jax.sharding import PartitionSpec as P


CAP = 24
IN_BLOCK = 256
OUT_BLOCK = 1024
COPY_BLOCK = 512
VMEM_BYTES = 67043328
FIRST = ("f0", "f1")
BATCHES = (("f0", "f1"), ("n",), ("f2", "f3"))
STAGES = (("f0", "f1"), ("n",), ("f2", "f3"))
ANY = pl.BlockSpec(memory_space=pl.ANY)
HBM = pl.BlockSpec(memory_space=pltpu.HBM)
VMEM = pl.BlockSpec(memory_space=pltpu.VMEM)


def token_slots(group_row, first_group, groups_here):
    tokens_here = group_row.shape[1]
    gid = lax.broadcasted_iota(jnp.int32, (groups_here, tokens_here), 0) + first_group
    starts = jnp.sum((group_row < gid).astype(jnp.int32), axis=1, keepdims=True)
    member = group_row == gid
    start = jnp.sum(jnp.where(member, starts, 0), axis=0, keepdims=True)
    slot = lax.broadcasted_iota(jnp.int32, (1, tokens_here), 1) - start
    return member, slot


def named_expert(member, lists, index):
    groups_here = member.shape[0]
    row = lists[index : index + 1, :]
    square = (groups_here, groups_here)
    diagonal = lax.broadcasted_iota(jnp.int32, square, 0) == lax.broadcasted_iota(jnp.int32, square, 1)
    column = jnp.sum(jnp.where(diagonal, jnp.broadcast_to(row, square), 0), axis=1, keepdims=True)
    return jnp.sum(jnp.where(member, column, 0), axis=0, keepdims=True)


def slot_hot(expert, slot, me, first, count, owners):
    place = ((expert ^ me) - first) & (owners - 1)
    key = jnp.where(expert >= 0, place * CAP + slot, -1)
    return lax.broadcasted_iota(jnp.int32, (count * CAP, key.shape[1]), 0) == key


def roomy(scratch):
    return scratch + 8 * 1024 * 1024


def block_rows(index):
    return pl.ds(index * CAP, CAP)


def column_blocks(width):
    block = min(width, COPY_BLOCK)
    return [pl.ds(at, block) for at in range(0, width, block)]


def start_all(copies):
    for copy in copies:
        copy.start()


def wait_all(copies):
    for copy in copies:
        copy.wait()


def pack_rows(experts, slot, me, first, owners, load, tokens_ref, outs):
    total = None
    for expert in experts:
        picks = slot_hot(expert, slot, me, first, sum(out.shape[0] for out in outs) // CAP, owners)
        total = picks if total is None else total | picks
    hot = total.astype(jnp.float32).astype(jnp.bfloat16)
    load.wait()
    for cols in column_blocks(tokens_ref.shape[1]):
        rows = jnp.dot(hot, tokens_ref[:, cols], preferred_element_type=jnp.float32)
        at = 0
        for out in outs:
            out[:, cols] = rows[at : at + out.shape[0]].astype(jnp.bfloat16)
            at += out.shape[0]


def pack_kernel(owners, first, count, group_hbm, lists_hbm, tokens_hbm, *refs):
    outs = refs[:count]
    group_ref, lists_ref, tokens_ref, sems = refs[count:]
    pairs = ((group_hbm, group_ref), (lists_hbm, lists_ref), (tokens_hbm, tokens_ref))
    loads = [pltpu.make_async_copy(source, target, sems.at[i]) for i, (source, target) in enumerate(pairs)]
    start_all(loads)
    wait_all(loads[:2])
    me = lax.axis_index("wide")
    groups_here = lists_ref.shape[1]
    member, slot = token_slots(group_ref[...], me * groups_here, groups_here)
    experts = [named_expert(member, lists_ref[...], j) for j in range(lists_ref.shape[0])]
    pack_rows(experts, slot, me, first, owners, loads[2], tokens_ref, outs)


def pack(group_row, lists, tokens, owners, first, heights):
    height, width = tokens.shape
    count = sum(heights) // CAP
    return pl.pallas_call(
        functools.partial(pack_kernel, owners, first, len(heights)),
        in_specs=[ANY] * 3,
        out_specs=[VMEM] * len(heights),
        scratch_shapes=[
            pltpu.VMEM(group_row.shape, group_row.dtype),
            pltpu.VMEM(lists.shape, lists.dtype),
            pltpu.VMEM((height, width), jnp.bfloat16),
            pltpu.SemaphoreType.DMA((3,)),
        ],
        out_shape=[pltpu.VMEM((rows, width), jnp.bfloat16) for rows in heights],
        cost_estimate=pl.CostEstimate(
            flops=2 * count * CAP * height * width,
            bytes_accessed=2 * width * (height + count * CAP),
            transcendentals=0,
        ),
        name="pack",
    )(group_row, lists, tokens)


def plan_kernel(owners, first, count, spans, group_ref, lists_ref, ids_ref, gates_ref, tokens_hbm, *refs):
    sources, refs = refs[:3], refs[3:]
    outs, refs = refs[:count], refs[count:]
    hots, refs = refs[: len(spans)], refs[len(spans) :]
    weight_ref, kept, (tokens_ref, token_sem, kept_sems) = refs[0], refs[1:4], refs[4:]
    load = pltpu.make_async_copy(tokens_hbm, tokens_ref, token_sem)
    keeps = [
        pltpu.make_async_copy(source, target, kept_sems.at[i]) for i, (source, target) in enumerate(zip(sources, kept))
    ]
    load.start()
    start_all(keeps)
    me = lax.axis_index("wide")
    groups_here = lists_ref.shape[1]
    member, slot = token_slots(group_ref[...], me * groups_here, groups_here)
    experts = [named_expert(member, lists_ref[...], j) for j in range(lists_ref.shape[0])]
    pack_rows(experts, slot, me, first, owners, load, tokens_ref, outs)
    for j, expert in enumerate(experts):
        gate = jnp.sum(jnp.where(ids_ref[...] == expert, gates_ref[...], 0.0), axis=0, keepdims=True)
        weight_ref[j] = jnp.transpose(jnp.broadcast_to(gate, (128, gate.shape[1])))
        for (start, length), hot in zip(spans, hots):
            picks = slot_hot(expert, slot, me, start, length, owners).astype(jnp.float32)
            hot[j] = jnp.transpose(picks).astype(jnp.bfloat16)
    wait_all(keeps)


def plan(group_row, lists, ids, gates, tokens, weights, owners, first, heights, spans):
    height, width = tokens.shape
    lists_long = lists.shape[0]
    return pl.pallas_call(
        functools.partial(plan_kernel, owners, first, len(heights), spans),
        in_specs=[VMEM] * 4 + [ANY] * 4,
        out_specs=[VMEM] * (len(heights) + len(spans) + 4),
        scratch_shapes=[
            pltpu.VMEM((height, width), jnp.bfloat16),
            pltpu.SemaphoreType.DMA,
            pltpu.SemaphoreType.DMA((len(weights),)),
        ],
        out_shape=[pltpu.VMEM((rows, width), jnp.bfloat16) for rows in heights]
        + [pltpu.VMEM((lists_long, height, length * CAP), jnp.bfloat16) for _, length in spans]
        + [pltpu.VMEM((lists_long, height, 128), jnp.float32)]
        + [pltpu.VMEM(weight.shape, weight.dtype) for weight in weights],
        cost_estimate=pl.CostEstimate(
            flops=2 * sum(heights) * height * width,
            bytes_accessed=sum(2 * weight.size for weight in weights),
            transcendentals=0,
        ),
        compiler_params=pltpu.CompilerParams(
            vmem_limit_bytes=VMEM_BYTES
            - sum(2 * weight.size for weight in weights)
            - 4 * owners * CAP * width
            - lists_long * height * (2 * owners * CAP + 512)
        ),
        name="plan",
    )(group_row, lists, ids, gates, tokens, *weights)


def gather_blocks(blocks, offsets, rows_ref):
    for i, (block, offset) in enumerate(zip(blocks, offsets)):
        rows_ref[block_rows(i)] = block[offset : offset + CAP]


def select_kernel(count, added, offsets, hot_ref, *refs):
    blocks, before, (out_ref, rows_ref) = refs[:count], refs[count : count + added], refs[count + added :]
    gather_blocks(blocks, offsets, rows_ref)
    for j in range(hot_ref.shape[0]):
        for cols in column_blocks(rows_ref.shape[1]):
            picked = jnp.dot(hot_ref[j], rows_ref[:, cols], preferred_element_type=jnp.float32)
            for other in before:
                picked = picked + other[j, :, cols].astype(jnp.float32)
            out_ref[j, :, cols] = picked.astype(jnp.bfloat16)


def select(hot, blocks, before):
    lists_long, height = hot.shape[:2]
    blocks, offsets = zip(*blocks)
    width = blocks[0].shape[1]
    return pl.pallas_call(
        functools.partial(select_kernel, len(blocks), len(before), offsets),
        in_specs=[VMEM] * (1 + len(blocks) + len(before)),
        out_specs=VMEM,
        scratch_shapes=[pltpu.VMEM((len(blocks) * CAP, width), jnp.bfloat16)],
        out_shape=pltpu.VMEM((lists_long, height, width), jnp.bfloat16),
        cost_estimate=pl.CostEstimate(
            flops=2 * hot.size * width, bytes_accessed=2 * len(blocks) * CAP * width, transcendentals=0
        ),
        compiler_params=pltpu.CompilerParams(
            vmem_limit_bytes=roomy(2 * (2 * len(blocks) * CAP * width + hot.size + 2 * lists_long * height * width))
        ),
        name="select",
    )(hot, *blocks, *before)


def mix_kernel(count, offsets, picked_ref, hot_ref, weight_ref, *refs):
    blocks = refs[:count]
    out_hbm, rows_ref, out_ref, sems = refs[count:]
    gather_blocks(blocks, offsets, rows_ref)
    stores = []
    for index, cols in enumerate(column_blocks(rows_ref.shape[1])):
        total = None
        for j in range(hot_ref.shape[0]):
            part = jnp.dot(hot_ref[j], rows_ref[:, cols], preferred_element_type=jnp.float32)
            part = part + picked_ref[j, :, cols].astype(jnp.float32)
            part = part * jnp.tile(weight_ref[j], (1, part.shape[1] // 128))
            total = part if total is None else total + part
        out_ref[:, cols] = total.astype(jnp.bfloat16)
        stores.append(pltpu.make_async_copy(out_ref.at[:, cols], out_hbm.at[:, cols], sems.at[index]))
        stores[-1].start()
    wait_all(stores)


def mix(picked, hot, weight, blocks):
    _, height, width = picked.shape
    blocks, offsets = zip(*blocks)
    return pl.pallas_call(
        functools.partial(mix_kernel, len(blocks), offsets),
        in_specs=[VMEM] * (3 + len(blocks)),
        out_specs=ANY,
        scratch_shapes=[
            pltpu.VMEM((len(blocks) * CAP, width), jnp.bfloat16),
            pltpu.VMEM((height, width), jnp.bfloat16),
            pltpu.SemaphoreType.DMA((len(column_blocks(width)),)),
        ],
        out_shape=jax.ShapeDtypeStruct((height, width), jnp.bfloat16),
        cost_estimate=pl.CostEstimate(
            flops=2 * hot.size * width, bytes_accessed=2 * height * width, transcendentals=0
        ),
        compiler_params=pltpu.CompilerParams(
            vmem_limit_bytes=roomy(
                2 * (2 * len(blocks) * CAP * width + height * width + hot.size + picked.size) + 4 * weight.size
            )
        ),
        name="mix",
    )(picked, hot, weight, *blocks)


def expert_kernel(offsets, narrow, wide, *refs):
    count = len(offsets)
    blocks = refs[:count]
    gate_ref, up_ref, down_ref = refs[count : count + 3]
    outs = refs[count + 3 : -2]
    rows_ref, hidden_ref = refs[-2:]
    width, inner = gate_ref.shape[1:]
    gather_blocks(blocks, offsets, rows_ref)
    for at in range(0, inner, narrow):
        cols = pl.ds(at, narrow)
        both = jnp.concatenate([gate_ref[0, :, cols], up_ref[0, :, cols]], axis=1)
        mixed = jnp.dot(rows_ref[...], both, preferred_element_type=jnp.float32)
        hidden = jax.nn.silu(mixed[:, :narrow]) * mixed[:, narrow:]
        hidden_ref[:, cols] = hidden.astype(jnp.bfloat16)
    for at in range(0, width, wide):
        cols = pl.ds(at, wide)
        result = jnp.dot(hidden_ref[...], down_ref[0, :, cols], preferred_element_type=jnp.float32)
        at = 0
        for out in outs:
            out[:, cols] = result[at : at + out.shape[0]].astype(jnp.bfloat16)
            at += out.shape[0]


def expert(blocks, heights, w_gate, w_up, w_down):
    blocks, offsets = zip(*blocks)
    count = len(blocks)
    width, inner = w_gate.shape[1:]
    narrow = min(inner, IN_BLOCK)
    wide = min(width, OUT_BLOCK)
    return pl.pallas_call(
        functools.partial(expert_kernel, offsets, narrow, wide),
        in_specs=[VMEM] * (count + 3),
        out_specs=[VMEM] * len(heights),
        scratch_shapes=[
            pltpu.VMEM((count * CAP, width), jnp.bfloat16),
            pltpu.VMEM((count * CAP, inner), jnp.bfloat16),
        ],
        out_shape=[pltpu.VMEM((rows, width), jnp.bfloat16) for rows in heights],
        cost_estimate=pl.CostEstimate(
            flops=6 * count * CAP * width * inner,
            bytes_accessed=4 * count * CAP * width,
            transcendentals=count * CAP * inner,
        ),
        compiler_params=pltpu.CompilerParams(vmem_limit_bytes=roomy(count * CAP * (4 * width + 2 * inner))),
        name="expert",
    )(*blocks, w_gate, w_up, w_down)


def swap(block, shift, owners):
    return lax.ppermute(block, "wide", [(i, i ^ shift) for i in range(owners)])


def heads_of(shifts, half):
    return [shift for shift in shifts if shift < half or shift % 2 == 0]


def heights_of(shifts, half):
    return [CAP if shift < half else 2 * CAP for shift in heads_of(shifts, half)]


def exchange(blocks, owners):
    half = owners // 2
    out = {}
    for shift, block in blocks.items():
        if shift == 0:
            out[0] = (block, 0)
            continue
        came = swap(block, shift, owners)
        out[shift] = (came, 0)
        if shift >= half:
            out[shift + 1] = (swap(came, 1, owners), CAP)
    return out


def shifts_of(owners):
    half = owners // 2
    far = list(range(half, owners))
    sets = {f"f{i}": far[len(far) * i // 4 : len(far) * (i + 1) // 4] for i in range(4)}
    sets["n"] = list(range(half))
    return sets


def joined(sets, names):
    return [shift for name in names for shift in sets[name]]


def on_device(tokens, token_group, group_experts, route_ids, route_gates, w_gate, w_up, w_down):
    owners = lax.axis_size("wide")
    assert owners & (owners - 1) == 0 and owners >= 8
    group_row = token_group.reshape(1, -1)
    lists = group_experts.T
    sets = shifts_of(owners)
    first = joined(sets, FIRST)
    rest = [(first[-1] + 1 + i) % owners for i in range(owners - len(first))]
    stages = [joined(sets, names) for names in STAGES]
    half = owners // 2
    sent = dict(
        zip(
            heads_of(first, half),
            pack(group_row, lists, tokens, owners, first[0], heights_of(first, half)),
        )
    )
    spans = tuple((stage[0], len(stage)) for stage in stages)
    made = plan(
        group_row,
        lists,
        route_ids.T,
        route_gates.T,
        tokens,
        (w_gate, w_up, w_down),
        owners,
        rest[0],
        heights_of(rest, half),
        spans,
    )
    heads = heads_of(rest, half)
    sent.update(zip(heads, made[: len(heads)]))
    hots, weight, weights = made[len(heads) : -4], made[-4], made[-3:]
    arrived = exchange(sent, owners)
    backs = {}
    for names in BATCHES:
        part = joined(sets, names)
        results = expert([arrived[shift] for shift in part], [CAP] * len(part), *weights)
        for shift, result in zip(part, results):
            backs[shift] = (swap(result, shift, owners) if shift else result, 0)
    picked = []
    for hot, stage in zip(hots[:-1], stages):
        picked = [select(hot, [backs[shift] for shift in stage], picked)]
    return mix(picked[0], hots[-1], weight, [backs[shift] for shift in stages[-1]])


def solution(mesh):
    in_specs = (
        P(("parts", "wide"), None),
        P(("parts", "wide")),
        P(("parts", "wide"), None),
        P(("parts", "wide"), None),
        P(("parts", "wide"), None),
        P("wide", None, None),
        P("wide", None, None),
        P("wide", None, None),
    )
    out_specs = P(("parts", "wide"), None)
    return jax.shard_map(
        on_device, mesh=mesh, in_specs=in_specs, out_specs=out_specs, check_vma=False
    )
```

```python
import functools

import jax
import jax.numpy as jnp
from jax import lax
from jax.experimental import pallas as pl
from jax.experimental.pallas import tpu as pltpu
from jax.sharding import PartitionSpec as P


CAP = 24
IN_BLOCK = 256
OUT_BLOCK = 1024
COPY_BLOCK = 512
VMEM_BYTES = 67043328
FIRST = ("f0", "f1")
BATCHES = (("f0", "f1"), ("n",), ("f2", "f3"))
STAGES = (("f0", "f1"), ("n",), ("f2", "f3"))
ANY = pl.BlockSpec(memory_space=pl.ANY)
HBM = pl.BlockSpec(memory_space=pltpu.HBM)
VMEM = pl.BlockSpec(memory_space=pltpu.VMEM)


def token_slots(group_row, first_group, groups_here):
    tokens_here = group_row.shape[1]
    gid = lax.broadcasted_iota(jnp.int32, (groups_here, tokens_here), 0) + first_group
    starts = jnp.sum((group_row < gid).astype(jnp.int32), axis=1, keepdims=True)
    member = group_row == gid
    start = jnp.sum(jnp.where(member, starts, 0), axis=0, keepdims=True)
    slot = lax.broadcasted_iota(jnp.int32, (1, tokens_here), 1) - start
    return member, slot


def named_expert(member, lists, index):
    groups_here = member.shape[0]
    row = lists[index : index + 1, :]
    square = (groups_here, groups_here)
    diagonal = lax.broadcasted_iota(jnp.int32, square, 0) == lax.broadcasted_iota(jnp.int32, square, 1)
    column = jnp.sum(jnp.where(diagonal, jnp.broadcast_to(row, square), 0), axis=1, keepdims=True)
    return jnp.sum(jnp.where(member, column, 0), axis=0, keepdims=True)


def slot_hot(expert, slot, me, first, count, owners):
    place = ((expert ^ me) - first) & (owners - 1)
    key = jnp.where(expert >= 0, place * CAP + slot, -1)
    return lax.broadcasted_iota(jnp.int32, (count * CAP, key.shape[1]), 0) == key


def roomy(scratch):
    return scratch + 8 * 1024 * 1024


def block_rows(index):
    return pl.ds(index * CAP, CAP)


def column_blocks(width):
    block = min(width, COPY_BLOCK)
    return [pl.ds(at, block) for at in range(0, width, block)]


def start_all(copies):
    for copy in copies:
        copy.start()


def wait_all(copies):
    for copy in copies:
        copy.wait()


def pack_rows(experts, slot, me, first, owners, loads, tokens_ref, outs):
    total = None
    for expert in experts:
        picks = slot_hot(expert, slot, me, first, sum(out.shape[0] for out in outs) // CAP, owners)
        total = picks if total is None else total | picks
    hot = total.astype(jnp.float32).astype(jnp.bfloat16)
    for index, cols in enumerate(column_blocks(tokens_ref.shape[1])):
        if index < len(loads):
            loads[index].wait()
        rows = jnp.dot(hot, tokens_ref[:, cols], preferred_element_type=jnp.float32)
        at = 0
        for out in outs:
            out[:, cols] = rows[at : at + out.shape[0]].astype(jnp.bfloat16)
            at += out.shape[0]


def pack_kernel(owners, first, count, group_hbm, lists_hbm, tokens_hbm, *refs):
    outs = refs[:count]
    group_ref, lists_ref, tokens_ref, sems = refs[count:]
    pairs = [(group_hbm, group_ref), (lists_hbm, lists_ref)]
    pairs += [(tokens_hbm.at[:, cols], tokens_ref.at[:, cols]) for cols in column_blocks(tokens_ref.shape[1])]
    loads = [pltpu.make_async_copy(source, target, sems.at[i]) for i, (source, target) in enumerate(pairs)]
    start_all(loads)
    wait_all(loads[:2])
    me = lax.axis_index("wide")
    groups_here = lists_ref.shape[1]
    member, slot = token_slots(group_ref[...], me * groups_here, groups_here)
    experts = [named_expert(member, lists_ref[...], j) for j in range(lists_ref.shape[0])]
    pack_rows(experts, slot, me, first, owners, loads[2:], tokens_ref, outs)


def pack(group_row, lists, tokens, owners, first, heights):
    height, width = tokens.shape
    count = sum(heights) // CAP
    return pl.pallas_call(
        functools.partial(pack_kernel, owners, first, len(heights)),
        in_specs=[ANY] * 3,
        out_specs=[VMEM] * len(heights),
        scratch_shapes=[
            pltpu.VMEM(group_row.shape, group_row.dtype),
            pltpu.VMEM(lists.shape, lists.dtype),
            pltpu.VMEM((height, width), jnp.bfloat16),
            pltpu.SemaphoreType.DMA((2 + len(column_blocks(width)),)),
        ],
        out_shape=[pltpu.VMEM((rows, width), jnp.bfloat16) for rows in heights],
        cost_estimate=pl.CostEstimate(
            flops=2 * count * CAP * height * width,
            bytes_accessed=2 * width * (height + count * CAP),
            transcendentals=0,
        ),
        name="pack",
    )(group_row, lists, tokens)


def plan_kernel(owners, first, count, spans, group_ref, lists_ref, ids_ref, gates_ref, tokens_hbm, *refs):
    sources, refs = refs[:3], refs[3:]
    outs, refs = refs[:count], refs[count:]
    hots, refs = refs[: len(spans)], refs[len(spans) :]
    weight_ref, kept, (tokens_ref, token_sem, kept_sems) = refs[0], refs[1:4], refs[4:]
    load = pltpu.make_async_copy(tokens_hbm, tokens_ref, token_sem)
    keeps = [
        pltpu.make_async_copy(source, target, kept_sems.at[i]) for i, (source, target) in enumerate(zip(sources, kept))
    ]
    load.start()
    start_all(keeps)
    me = lax.axis_index("wide")
    groups_here = lists_ref.shape[1]
    member, slot = token_slots(group_ref[...], me * groups_here, groups_here)
    experts = [named_expert(member, lists_ref[...], j) for j in range(lists_ref.shape[0])]
    pack_rows(experts, slot, me, first, owners, [load], tokens_ref, outs)
    for j, expert in enumerate(experts):
        gate = jnp.sum(jnp.where(ids_ref[...] == expert, gates_ref[...], 0.0), axis=0, keepdims=True)
        weight_ref[j] = jnp.transpose(jnp.broadcast_to(gate, (128, gate.shape[1])))
        for (start, length), hot in zip(spans, hots):
            picks = slot_hot(expert, slot, me, start, length, owners).astype(jnp.float32)
            hot[j] = jnp.transpose(picks).astype(jnp.bfloat16)
    wait_all(keeps)


def plan(group_row, lists, ids, gates, tokens, weights, owners, first, heights, spans):
    height, width = tokens.shape
    lists_long = lists.shape[0]
    return pl.pallas_call(
        functools.partial(plan_kernel, owners, first, len(heights), spans),
        in_specs=[VMEM] * 4 + [ANY] * 4,
        out_specs=[VMEM] * (len(heights) + len(spans) + 4),
        scratch_shapes=[
            pltpu.VMEM((height, width), jnp.bfloat16),
            pltpu.SemaphoreType.DMA,
            pltpu.SemaphoreType.DMA((len(weights),)),
        ],
        out_shape=[pltpu.VMEM((rows, width), jnp.bfloat16) for rows in heights]
        + [pltpu.VMEM((lists_long, height, length * CAP), jnp.bfloat16) for _, length in spans]
        + [pltpu.VMEM((lists_long, height, 128), jnp.float32)]
        + [pltpu.VMEM(weight.shape, weight.dtype) for weight in weights],
        cost_estimate=pl.CostEstimate(
            flops=2 * sum(heights) * height * width,
            bytes_accessed=sum(2 * weight.size for weight in weights),
            transcendentals=0,
        ),
        compiler_params=pltpu.CompilerParams(
            vmem_limit_bytes=VMEM_BYTES
            - sum(2 * weight.size for weight in weights)
            - 4 * owners * CAP * width
            - lists_long * height * (2 * owners * CAP + 512)
        ),
        name="plan",
    )(group_row, lists, ids, gates, tokens, *weights)


def gather_blocks(blocks, offsets, rows_ref):
    for i, (block, offset) in enumerate(zip(blocks, offsets)):
        rows_ref[block_rows(i)] = block[offset : offset + CAP]


def select_kernel(count, added, offsets, hot_ref, *refs):
    blocks, before, (out_ref, rows_ref) = refs[:count], refs[count : count + added], refs[count + added :]
    gather_blocks(blocks, offsets, rows_ref)
    for j in range(hot_ref.shape[0]):
        for cols in column_blocks(rows_ref.shape[1]):
            picked = jnp.dot(hot_ref[j], rows_ref[:, cols], preferred_element_type=jnp.float32)
            for other in before:
                picked = picked + other[j, :, cols].astype(jnp.float32)
            out_ref[j, :, cols] = picked.astype(jnp.bfloat16)


def select(hot, blocks, before):
    lists_long, height = hot.shape[:2]
    blocks, offsets = zip(*blocks)
    width = blocks[0].shape[1]
    return pl.pallas_call(
        functools.partial(select_kernel, len(blocks), len(before), offsets),
        in_specs=[VMEM] * (1 + len(blocks) + len(before)),
        out_specs=VMEM,
        scratch_shapes=[pltpu.VMEM((len(blocks) * CAP, width), jnp.bfloat16)],
        out_shape=pltpu.VMEM((lists_long, height, width), jnp.bfloat16),
        cost_estimate=pl.CostEstimate(
            flops=2 * hot.size * width, bytes_accessed=2 * len(blocks) * CAP * width, transcendentals=0
        ),
        compiler_params=pltpu.CompilerParams(
            vmem_limit_bytes=roomy(2 * (2 * len(blocks) * CAP * width + hot.size + 2 * lists_long * height * width))
        ),
        name="select",
    )(hot, *blocks, *before)


def mix_kernel(count, offsets, picked_ref, hot_ref, weight_ref, *refs):
    blocks = refs[:count]
    out_hbm, rows_ref, out_ref, sems = refs[count:]
    gather_blocks(blocks, offsets, rows_ref)
    stores = []
    for index, cols in enumerate(column_blocks(rows_ref.shape[1])):
        total = None
        for j in range(hot_ref.shape[0]):
            part = jnp.dot(hot_ref[j], rows_ref[:, cols], preferred_element_type=jnp.float32)
            part = part + picked_ref[j, :, cols].astype(jnp.float32)
            part = part * jnp.tile(weight_ref[j], (1, part.shape[1] // 128))
            total = part if total is None else total + part
        out_ref[:, cols] = total.astype(jnp.bfloat16)
        stores.append(pltpu.make_async_copy(out_ref.at[:, cols], out_hbm.at[:, cols], sems.at[index]))
        stores[-1].start()
    wait_all(stores)


def mix(picked, hot, weight, blocks):
    _, height, width = picked.shape
    blocks, offsets = zip(*blocks)
    return pl.pallas_call(
        functools.partial(mix_kernel, len(blocks), offsets),
        in_specs=[VMEM] * (3 + len(blocks)),
        out_specs=ANY,
        scratch_shapes=[
            pltpu.VMEM((len(blocks) * CAP, width), jnp.bfloat16),
            pltpu.VMEM((height, width), jnp.bfloat16),
            pltpu.SemaphoreType.DMA((len(column_blocks(width)),)),
        ],
        out_shape=jax.ShapeDtypeStruct((height, width), jnp.bfloat16),
        cost_estimate=pl.CostEstimate(
            flops=2 * hot.size * width, bytes_accessed=2 * height * width, transcendentals=0
        ),
        compiler_params=pltpu.CompilerParams(
            vmem_limit_bytes=roomy(
                2 * (2 * len(blocks) * CAP * width + height * width + hot.size + picked.size) + 4 * weight.size
            )
        ),
        name="mix",
    )(picked, hot, weight, *blocks)


def expert_kernel(offsets, narrow, wide, *refs):
    count = len(offsets)
    blocks = refs[:count]
    gate_ref, up_ref, down_ref = refs[count : count + 3]
    outs = refs[count + 3 : -2]
    rows_ref, hidden_ref = refs[-2:]
    width, inner = gate_ref.shape[1:]
    gather_blocks(blocks, offsets, rows_ref)
    for at in range(0, inner, narrow):
        cols = pl.ds(at, narrow)
        both = jnp.concatenate([gate_ref[0, :, cols], up_ref[0, :, cols]], axis=1)
        mixed = jnp.dot(rows_ref[...], both, preferred_element_type=jnp.float32)
        hidden = jax.nn.silu(mixed[:, :narrow]) * mixed[:, narrow:]
        hidden_ref[:, cols] = hidden.astype(jnp.bfloat16)
    for at in range(0, width, wide):
        cols = pl.ds(at, wide)
        result = jnp.dot(hidden_ref[...], down_ref[0, :, cols], preferred_element_type=jnp.float32)
        at = 0
        for out in outs:
            out[:, cols] = result[at : at + out.shape[0]].astype(jnp.bfloat16)
            at += out.shape[0]


def expert(blocks, heights, w_gate, w_up, w_down):
    blocks, offsets = zip(*blocks)
    count = len(blocks)
    width, inner = w_gate.shape[1:]
    narrow = min(inner, IN_BLOCK)
    wide = min(width, OUT_BLOCK)
    return pl.pallas_call(
        functools.partial(expert_kernel, offsets, narrow, wide),
        in_specs=[VMEM] * (count + 3),
        out_specs=[VMEM] * len(heights),
        scratch_shapes=[
            pltpu.VMEM((count * CAP, width), jnp.bfloat16),
            pltpu.VMEM((count * CAP, inner), jnp.bfloat16),
        ],
        out_shape=[pltpu.VMEM((rows, width), jnp.bfloat16) for rows in heights],
        cost_estimate=pl.CostEstimate(
            flops=6 * count * CAP * width * inner,
            bytes_accessed=4 * count * CAP * width,
            transcendentals=count * CAP * inner,
        ),
        compiler_params=pltpu.CompilerParams(vmem_limit_bytes=roomy(count * CAP * (4 * width + 2 * inner))),
        name="expert",
    )(*blocks, w_gate, w_up, w_down)


def swap(block, shift, owners):
    return lax.ppermute(block, "wide", [(i, i ^ shift) for i in range(owners)])


def heads_of(shifts, half):
    return [shift for shift in shifts if shift < half or shift % 2 == 0]


def heights_of(shifts, half):
    return [CAP if shift < half else 2 * CAP for shift in heads_of(shifts, half)]


def exchange(blocks, owners):
    half = owners // 2
    out = {}
    for shift, block in blocks.items():
        if shift == 0:
            out[0] = (block, 0)
            continue
        came = swap(block, shift, owners)
        out[shift] = (came, 0)
        if shift >= half:
            out[shift + 1] = (swap(came, 1, owners), CAP)
    return out


def shifts_of(owners):
    half = owners // 2
    far = list(range(half, owners))
    sets = {f"f{i}": far[len(far) * i // 4 : len(far) * (i + 1) // 4] for i in range(4)}
    sets["n"] = list(range(half))
    return sets


def joined(sets, names):
    return [shift for name in names for shift in sets[name]]


def on_device(tokens, token_group, group_experts, route_ids, route_gates, w_gate, w_up, w_down):
    owners = lax.axis_size("wide")
    assert owners & (owners - 1) == 0 and owners >= 8
    group_row = token_group.reshape(1, -1)
    lists = group_experts.T
    sets = shifts_of(owners)
    first = joined(sets, FIRST)
    rest = [(first[-1] + 1 + i) % owners for i in range(owners - len(first))]
    stages = [joined(sets, names) for names in STAGES]
    half = owners // 2
    sent = dict(
        zip(
            heads_of(first, half),
            pack(group_row, lists, tokens, owners, first[0], heights_of(first, half)),
        )
    )
    spans = tuple((stage[0], len(stage)) for stage in stages)
    made = plan(
        group_row,
        lists,
        route_ids.T,
        route_gates.T,
        tokens,
        (w_gate, w_up, w_down),
        owners,
        rest[0],
        heights_of(rest, half),
        spans,
    )
    heads = heads_of(rest, half)
    sent.update(zip(heads, made[: len(heads)]))
    hots, weight, weights = made[len(heads) : -4], made[-4], made[-3:]
    arrived = exchange(sent, owners)
    backs = {}
    for names in BATCHES:
        part = joined(sets, names)
        results = expert([arrived[shift] for shift in part], [CAP] * len(part), *weights)
        for shift, result in zip(part, results):
            backs[shift] = (swap(result, shift, owners) if shift else result, 0)
    picked = []
    for hot, stage in zip(hots[:-1], stages):
        picked = [select(hot, [backs[shift] for shift in stage], picked)]
    return mix(picked[0], hots[-1], weight, [backs[shift] for shift in stages[-1]])


def solution(mesh):
    in_specs = (
        P(("parts", "wide"), None),
        P(("parts", "wide")),
        P(("parts", "wide"), None),
        P(("parts", "wide"), None),
        P(("parts", "wide"), None),
        P("wide", None, None),
        P("wide", None, None),
        P("wide", None, None),
    )
    out_specs = P(("parts", "wide"), None)
    return jax.shard_map(
        on_device, mesh=mesh, in_specs=in_specs, out_specs=out_specs, check_vma=False
    )
```
